128 devices in a mesh: fsdp: 32 (over z, y, core), slide: 4 (over x).
Axes of the slice: x: 4, y: 4, z: 4, core: 2. Of those that a mesh axis runs over, the one named last changes fastest.
Arguments:
- tiles: bfloat16 [65536, 1536], P(('slide', 'fsdp')), parts along dimension 0, may hold values from -6 to 6
- tile_cell: int32 [65536], P('slide'), parts along dimension 0, may hold values from 0 to 16383, as said below
- tissue: int32 [256, 256], P('slide'), parts along dimension 0, may hold values 0 or 1
- norm_gain: float32 [2, 1536], replicated, may hold values from 0.5 to 1.5
- qk_gain: float32 [2, 2, 64], replicated, may hold values from 0.5 to 4
- row_qkv: bfloat16 [1536, 4608], P(None, 'fsdp'), may hold values from -0.15625 to 0.15625
- row_out: bfloat16 [1536, 1536], P(None, 'fsdp'), may hold values from -0.15625 to 0.15625
- col_qkv: bfloat16 [1536, 4608], P(None, 'fsdp'), may hold values from -0.15625 to 0.15625
- col_out: bfloat16 [1536, 1536], P(None, 'fsdp'), may hold values from -0.15625 to 0.15625
Outputs:
- encoded: bfloat16 [256, 256, 1536], P('slide', 'fsdp'), parts along dimension 0
The draws below stay inside these ranges and needn't reach their ends.
There are 4 independent parts, one for each index of `slide`. The reference program is written for one: setup_inputs(seed, part) draws one part's arguments, and reference() takes and returns one part's arrays. A program takes and returns all parts, laid end to end along the dimension named above; an argument that names none is the same for every part. Nothing has to cross between parts.
Inputs may be any that keep to these rules, and one draw needn't show every extreme that they name: Slots d * 512 + b * 16 up to d * 512 + (b + 1) * 16 - 1 hold tiles of grid rows b * 2 to (b + 1) * 2 - 1; tile_cell names every grid cell exactly once.
All inputs are finite; a program needn't handle non-finite values.
Results may differ from the reference program's by a relative error of at most 0.02.
The reference program's roundings to bfloat16 on the way count: a program that leaves them out, or rounds other values in their place, can miss the bound.
Values may be sent and summed in bfloat16 or wider, within the bound.
No kernel may reach another device: no remote copies, remote signals or barrier semaphores. Data moves between devices by JAX's collectives and lax.ppermute only.
A program may use at most 256 MiB of HBM per device.

```python
import jax
import jax.numpy as jnp
from jax import lax

D = 1536
HEADS = 24
HS = 64
COLS = 256
ROWS_DEV = 2
GRID_R = 64
TOKENS = 16384
N_FSDP = 32


def draw_tile_cell(key, part):
    count = N_FSDP
    tok_dev = ROWS_DEV * COLS
    slots = tok_dev // count
    scores = jax.random.randint(jax.random.fold_in(key, 7), (count, tok_dev), 0, 65536) * tok_dev
    scores = scores + jnp.arange(tok_dev, dtype=jnp.int32)[None, :]
    local = jnp.argsort(scores, axis=1, stable=True).astype(jnp.int32)
    cells = jnp.arange(count, dtype=jnp.int32)[:, None] * tok_dev + local
    cells = cells.reshape(count, count, slots).transpose(1, 0, 2).reshape(-1)
    return cells.astype(jnp.int32)


def draw_qk_gain(key, part):
    values = jax.random.uniform(jax.random.fold_in(key, 11), (2, 2, HS), jnp.float32, 0.6, 1.4)
    return values.astype(jnp.float32)


def touch_ends(array, rng, low, largest):
    extent = array.shape
    index_at = [jax.random.randint(jax.random.fold_in(rng, axis), (), 0, extent[axis]) for axis in range(len(extent))]
    array = array.at[tuple(index_at)].set(low)
    longest = extent.index(max(extent))
    index_at[longest] = (index_at[longest] + 1) % extent[longest]
    return array.at[tuple(index_at)].set(largest)


def block_scale(stream_key, dims, shards, low, top_value):
    factor_of, own = 1.0, jax.random.fold_in(stream_key, 6)
    for dim, shards_of in shards:
        steps = jnp.exp(jax.random.uniform(jax.random.fold_in(own, dim), (shards_of,), jnp.float32, low / len(shards), top_value / len(shards)))
        factor_of = factor_of * jnp.repeat(steps, dims[dim] // shards_of).reshape([-1 if axis == dim else 1 for axis in range(len(dims))])
    return factor_of


def noise(rng, shape, spread, most, pieces=(), kind=jnp.bfloat16):
    values = spread * jax.random.normal(rng, shape, jnp.float32)
    if pieces:
        values = values * block_scale(rng, shape, pieces, -0.22, 0.18)
    return jnp.clip(values, -most, most).astype(kind)


def setup_inputs(seed: int = 0, part: int = 0) -> dict:
    splits = jax.random.split(jax.random.key(seed), 10)
    part_keys = jax.random.split(jax.random.fold_in(splits[9], part), 10)
    return {
        "tiles": noise(part_keys[0], (TOKENS, D), 1.0, 6.0, ((0, 32),)),
        "tile_cell": draw_tile_cell(jax.random.fold_in(jax.random.fold_in(splits[9], part), 71), part),
        "tissue": touch_ends((jax.random.randint(part_keys[2], (GRID_R, COLS), 0, 5) < 3).astype(jnp.int32), jax.random.fold_in(part_keys[2], 1), 0, 1),
        "norm_gain": jnp.clip(1.0 + 0.1 * jax.random.normal(splits[3], (2, D), jnp.float32), 0.5, 1.5),
        "qk_gain": draw_qk_gain(jax.random.fold_in(splits[9], 71), part),
        "row_qkv": noise(splits[5], (D, 3 * D), D ** -0.5, 0.15625, ((1, 32),)),
        "row_out": noise(splits[6], (D, D), D ** -0.5, 0.15625, ((1, 32),)),
        "col_qkv": noise(splits[7], (D, 3 * D), D ** -0.5, 0.15625, ((1, 32),)),
        "col_out": noise(splits[8], (D, D), D ** -0.5, 0.15625, ((1, 32),)),
    }


EPS = 1e-06

def rms_norm(grid, gain):
    values = grid.astype(jnp.float32)
    scale = lax.rsqrt(lax.optimization_barrier(jnp.mean(values * values, axis=-1, keepdims=True)) + EPS)
    return (values * scale * gain).astype(jnp.bfloat16)

def head_norm(values, gain):
    scale = lax.rsqrt(lax.optimization_barrier(jnp.mean(values * values, axis=-1, keepdims=True)) + EPS)
    return values * scale * gain

def rotate(values, rows_pos, cols_pos):
    quarter = values.shape[-1] // 4
    freq = 10000.0 ** (-jnp.arange(quarter).astype(jnp.float32) / quarter)

    def turn(part, position):
        angle = position.astype(jnp.float32)[..., None, None] * freq
        cosine = jnp.cos(angle)
        sine = jnp.sin(angle)
        first = part[..., :quarter]
        second = part[..., quarter:]
        return jnp.concatenate([first * cosine - second * sine, first * sine + second * cosine], axis=-1)
    half = 2 * quarter
    return jnp.concatenate([turn(values[..., :half], rows_pos), turn(values[..., half:], cols_pos)], axis=-1)

def attend(qkv, gains, rows_pos, cols_pos, keys_live, column, heads):
    width = qkv.shape[-1] // 3
    size = width // heads
    shape = qkv.shape[:-1] + (heads, size)
    query = qkv[..., :width].reshape(shape).astype(jnp.float32)
    key = qkv[..., width:2 * width].reshape(shape).astype(jnp.float32)
    value = qkv[..., 2 * width:].reshape(shape).astype(jnp.float32)
    query = lax.optimization_barrier(rotate(head_norm(query, gains[0]), rows_pos, cols_pos).astype(jnp.bfloat16))
    key = lax.optimization_barrier(rotate(head_norm(key, gains[1]), rows_pos, cols_pos).astype(jnp.bfloat16))
    if column:
        score_form = 'lbhd,mbhd->bhlm'
        mix_form = 'bhlm,mbhd->lbhd'
        live = keys_live.T
    else:
        score_form = 'blhd,bmhd->bhlm'
        mix_form = 'bhlm,bmhd->blhd'
        live = keys_live
    scores = jnp.einsum(score_form, query.astype(jnp.float32), key.astype(jnp.float32)) * size ** (-0.5)
    length = scores.shape[-1]
    diagonal = jnp.arange(length)[:, None] == jnp.arange(length)[None, :]
    allow = (live[:, None, None, :] > 0) | diagonal[None, None]
    scores = jnp.where(allow, scores, -1e+30)
    top = lax.optimization_barrier(jnp.max(scores, axis=-1, keepdims=True))
    weights = jnp.exp(scores - top)
    total = lax.optimization_barrier(jnp.sum(weights, axis=-1))
    rounded = lax.optimization_barrier(weights.astype(jnp.bfloat16))
    mixed = jnp.einsum(mix_form, rounded.astype(jnp.float32), value)
    if column:
        total = total.transpose(2, 0, 1)
    else:
        total = total.transpose(0, 2, 1)
    return (mixed / total[..., None]).reshape(qkv.shape[:-1] + (width,)).astype(jnp.bfloat16)

def reference(tiles, tile_cell, tissue, norm_gain, qk_gain, row_qkv, row_out, col_qkv, col_out):
    cells = tile_cell.astype(jnp.int32)
    grid = jnp.zeros((TOKENS, D), jnp.bfloat16).at[cells].set(tiles)
    rows_pos = lax.broadcasted_iota(jnp.int32, (GRID_R, COLS), 0)
    cols_pos = lax.broadcasted_iota(jnp.int32, (GRID_R, COLS), 1)
    qkv = jnp.dot(rms_norm(grid, norm_gain[0]), row_qkv, preferred_element_type=jnp.float32)
    qkv = qkv.astype(jnp.bfloat16).reshape(GRID_R, COLS, 3 * D)

    def one_row(items):
        line, row_p, col_p, live = items
        return attend(line[None], qk_gain[0], row_p[None], col_p[None], live[None], False, HEADS)[0]
    mixed = lax.map(one_row, (qkv, rows_pos, cols_pos, tissue))
    hidden = grid.astype(jnp.float32) + jnp.dot(mixed.reshape(TOKENS, D), row_out, preferred_element_type=jnp.float32)
    hidden = hidden.astype(jnp.bfloat16)
    qkv_col = jnp.dot(rms_norm(hidden, norm_gain[1]), col_qkv, preferred_element_type=jnp.float32)
    qkv_col = qkv_col.astype(jnp.bfloat16).reshape(GRID_R, COLS, 3 * D)
    mixed_col = attend(qkv_col, qk_gain[1], rows_pos, cols_pos, tissue, True, HEADS)
    result = hidden.astype(jnp.float32) + jnp.dot(mixed_col.reshape(TOKENS, D), col_out, preferred_element_type=jnp.float32)
    return result.astype(jnp.bfloat16).reshape(GRID_R, COLS, D)
```

```python
import functools

import jax
import jax.numpy as jnp
from jax import lax
from jax.experimental import pallas as pl
from jax.experimental.pallas import tpu as pltpu
from jax.sharding import PartitionSpec as P

HEADS = 24
SIZE = 64
EPS = 1e-06
F32 = jnp.float32
BF16 = jnp.bfloat16
NT = (((1,), (1,)), ((), ()))


def params(mib):
    return pltpu.CompilerParams(vmem_limit_bytes=mib * 1024 * 1024)


def one_hot(hot, order_row):
    rows = lax.broadcasted_iota(jnp.int32, (hot, hot), 0)
    return (rows == order_row).astype(BF16)


def select(matrix, values):
    return jnp.dot(matrix, values, preferred_element_type=F32)


def normed(values, gain):
    scale = lax.rsqrt(jnp.mean(values * values, axis=-1, keepdims=True) + EPS)
    return (values * scale * gain).astype(BF16)


def enter_kernel(send_ref, row_ref, gain_ref, tiles_ref, x_ref, xn_ref):
    tiles = tiles_ref[...]
    hot = tiles.shape[0]
    x_ref[...] = select(one_hot(hot, send_ref[...]), tiles).astype(BF16)
    xn_ref[...] = normed(select(one_hot(hot, row_ref[...]), tiles), gain_ref[...])


def turn_kernel(order_ref, gain_ref, h_ref, xn_ref):
    xn = normed(h_ref[...].astype(F32), gain_ref[...])
    xn_ref[...] = select(one_hot(xn.shape[0], order_ref[...]), xn).astype(BF16)


def qkv_kernel(w_ref, xn_ref, out_ref):
    blocks, rows, width = w_ref.shape
    w = w_ref[...].reshape(blocks * rows, width)
    out_ref[...] = lax.dot_general(w, xn_ref[...], NT, preferred_element_type=F32).astype(BF16)


def swap_halves(t):
    return jnp.concatenate([t[16:32], t[:16], t[48:64], t[32:48]], axis=0)


def turned(t, cos, sin, factor):
    scale = lax.rsqrt(jnp.mean(t * t, axis=0, keepdims=True) + EPS) * factor
    return (t * cos + swap_halves(t) * sin) * scale


def attend_kernel(q_ref, k_ref, v_ref, cq_ref, sq_ref, ck_ref, sk_ref, bias_ref, out_ref):
    groups, keys, _ = bias_ref.shape
    for head in range(q_ref.shape[0] // SIZE):
        at = slice(head * SIZE, (head + 1) * SIZE)
        q = turned(q_ref[at, :].astype(F32), cq_ref[...], sq_ref[...], SIZE**-0.5).astype(BF16)
        k = turned(k_ref[at, :].astype(F32), ck_ref[...], sk_ref[...], 1.0)
        k = k.T.astype(BF16)
        v = v_ref[at, :]
        for group in range(groups):
            line = slice(group * keys, (group + 1) * keys)
            s = jnp.dot(k[line], q[:, line], preferred_element_type=F32) + bias_ref[group]
            w = jnp.exp(s - jnp.max(s, axis=0, keepdims=True))
            total = jnp.sum(w, axis=0, keepdims=True)
            mixed = jnp.dot(v[:, line], w.astype(BF16), preferred_element_type=F32)
            out_ref[at, line] = (mixed * (1.0 / total)).astype(BF16)


def out_kernel(order_ref, w_ref, mixed_ref, x_ref, out_ref, held_ref):
    @pl.when(pl.program_id(0) == 0)
    def _():
        pick = one_hot(mixed_ref.shape[1], order_ref[...])
        held_ref[...] = lax.dot_general(pick, mixed_ref[...], NT, preferred_element_type=F32).astype(BF16)

    blocks, rows, width = w_ref.shape
    w = w_ref[...].reshape(blocks * rows, width)
    add = lax.dot_general(held_ref[...], w, NT, preferred_element_type=F32)
    out_ref[...] = (x_ref[...].astype(F32) + add).astype(BF16)


def enter(tiles, send_order, row_order, gain):
    shape = jax.ShapeDtypeStruct(tiles.shape, BF16)
    return pl.pallas_call(
        enter_kernel, out_shape=(shape, shape), compiler_params=params(40), name="enter"
    )(send_order, row_order, gain, tiles)


def turn(h, order, gain):
    return pl.pallas_call(
        turn_kernel, out_shape=jax.ShapeDtypeStruct(h.shape, BF16), compiler_params=params(40), name="turn"
    )(order, gain, h)


def qkv_of(weights, xn):
    parts, _, width = weights.shape
    tokens = xn.shape[0]
    step, rows = 4, 3 * width // parts
    return pl.pallas_call(
        qkv_kernel,
        grid=(parts // step,),
        in_specs=[
            pl.BlockSpec((step, rows, width), lambda i: (i, 0, 0)),
            pl.BlockSpec((tokens, width), lambda i: (0, 0)),
        ],
        out_specs=pl.BlockSpec((step * rows, tokens), lambda i: (i, 0)),
        out_shape=jax.ShapeDtypeStruct((3 * width, tokens), BF16),
        compiler_params=params(40),
        name="qkv",
    )(weights, xn)


def attend(qkv, tables, bias, heads_step):
    width3, tokens = qkv.shape
    rows = heads_step * SIZE
    steps = HEADS // heads_step

    def part(j):
        return pl.BlockSpec((rows, tokens), lambda i, j=j: (j * steps + i, 0))

    table = pl.BlockSpec((SIZE, tokens), lambda i: (0, 0))
    return pl.pallas_call(
        attend_kernel,
        grid=(steps,),
        in_specs=[part(0), part(1), part(2), table, table, table, table, pl.BlockSpec(bias.shape, lambda i: (0, 0, 0))],
        out_specs=part(0),
        out_shape=jax.ShapeDtypeStruct((width3 // 3, tokens), BF16),
        compiler_params=params(40),
        name="attend",
    )(qkv, qkv, qkv, *tables, bias)


def out_of(weights, mixed, x, order):
    parts, rows4, width = weights.shape
    tokens = x.shape[0]
    step, rows = 8, rows4 // 4
    return pl.pallas_call(
        out_kernel,
        grid=(parts // step,),
        in_specs=[
            pl.BlockSpec((1, tokens), lambda i: (0, 0)),
            pl.BlockSpec((step, rows, width), lambda i: (i, 3, 0)),
            pl.BlockSpec((width, tokens), lambda i: (0, 0)),
            pl.BlockSpec((tokens, step * rows), lambda i: (0, i)),
        ],
        out_specs=pl.BlockSpec((tokens, step * rows), lambda i: (0, i)),
        out_shape=jax.ShapeDtypeStruct((tokens, width), BF16),
        scratch_shapes=[pltpu.VMEM((tokens, width), BF16)],
        compiler_params=params(40),
        name="project",
    )(order, weights, mixed, x)


def rotary_tables(gains, rows_pos, cols_pos):
    quarter = SIZE // 4
    freq = 10000.0 ** (-jnp.arange(quarter).astype(F32) / quarter)
    by_row = freq[:, None] * rows_pos.astype(F32)[None, :]
    by_col = freq[:, None] * cols_pos.astype(F32)[None, :]
    cr, sr, cc, sc = jnp.cos(by_row), jnp.sin(by_row), jnp.cos(by_col), jnp.sin(by_col)
    cosine = jnp.concatenate([cr, cr, cc, cc], axis=0)
    sine = jnp.concatenate([-sr, sr, -sc, sc], axis=0)
    out = []
    for gain in (gains[0], gains[1]):
        other = jnp.concatenate([gain[16:32], gain[:16], gain[48:64], gain[32:48]])
        out += [gain[:, None] * cosine, other[:, None] * sine]
    return out


def on_device(tiles, tile_cell, tissue, norm_gain, qk_gain, row_qkv, row_out, col_qkv, col_out):
    count = lax.axis_size("fsdp")
    index = lax.axis_index("fsdp")
    tokens, width = tiles.shape
    slots = tokens // count
    grid_rows, columns = tissue.shape
    rows_dev = grid_rows // count
    cols_dev = columns // count

    def gather(qkv, out):
        return lax.all_gather(jnp.concatenate([qkv.T, out.T], axis=0), "fsdp", axis=0, tiled=False)

    row_w = gather(row_qkv, row_out)
    col_w = gather(col_qkv, col_out)

    arrived = lax.all_to_all(
        tiles.reshape(count, slots, width), "fsdp", split_axis=0, concat_axis=0, tiled=True
    ).reshape(tokens, width)
    table_cell = lax.dynamic_index_in_dim(tile_cell.reshape(count, count, slots), index, 1, keepdims=False)
    row_base = index * rows_dev
    col_base = index * cols_dev
    local = (table_cell - row_base * columns).reshape(1, tokens)
    r, c = local // columns, local % columns
    send = (c // cols_dev) * (rows_dev * cols_dev) + r * cols_dev + c % cols_dev

    token = jnp.arange(tokens, dtype=jnp.int32)
    row_tables = rotary_tables(qk_gain[0], row_base + token // columns, token % columns)
    live = lax.dynamic_slice_in_dim(tissue, row_base, rows_dev, 0) > 0
    at = jnp.arange(columns)
    allow = live[:, :, None] | (at[:, None] == at[None, :])[None]
    row_bias = jnp.where(allow, 0.0, -1e30).astype(F32)

    x, xn = enter(arrived, send, local, norm_gain[0:1])
    mixed = attend(qkv_of(row_w, xn), row_tables, row_bias, 2)
    t_c, t_r = token % columns, token // columns
    send_of_row = (t_c // cols_dev) * (rows_dev * cols_dev) + t_r * cols_dev + t_c % cols_dev
    h = out_of(row_w, mixed, x, send_of_row[None, :])
    flat = lax.all_to_all(
        h.reshape(count, slots, width), "fsdp", split_axis=0, concat_axis=0, tiled=True
    ).reshape(tokens, width)

    turned_of = (token % cols_dev) * grid_rows + token // cols_dev
    back_of = (token % grid_rows) * cols_dev + token // grid_rows
    col_tables = rotary_tables(qk_gain[1], token % grid_rows, col_base + token // grid_rows)
    live = lax.dynamic_slice_in_dim(tissue, col_base, cols_dev, 1).T.reshape(-1) > 0
    pair = 2 * grid_rows
    at = jnp.arange(pair)
    same = (at[:, None] // grid_rows) == (at[None, :] // grid_rows)
    allow = (live.reshape(-1, pair)[:, :, None] & same[None]) | (at[:, None] == at[None, :])[None]
    col_bias = jnp.where(allow, 0.0, -1e30).astype(F32)

    xn = turn(flat, turned_of[None, :], norm_gain[1:2])
    mixed = attend(qkv_of(col_w, xn), col_tables, col_bias, 2)
    result = out_of(col_w, mixed, flat, back_of[None, :])
    return result.reshape(grid_rows, cols_dev, width)


def solution(mesh):
    return jax.shard_map(
        on_device,
        mesh=mesh,
        in_specs=(
            P(("slide", "fsdp"), None),
            P("slide"),
            P("slide", None),
            P(),
            P(),
            P(None, "fsdp"),
            P(None, "fsdp"),
            P(None, "fsdp"),
            P(None, "fsdp"),
        ),
        out_specs=P("slide", "fsdp", None),
        check_vma=False,
    )
```
